32 devices in a mesh: rows: 8 (over y, x, core), dict: 4 (over z).
Axes of the slice: x: 2, y: 2, z: 4, core: 2. Of those that a mesh axis runs over, the one named last changes fastest.
Arguments:
- lookup_keys_per_record: int32 [131072], P(('rows', 'dict')), may hold values from 0 to 32767, as said below
- filter_passed_flags: int32 [131072], P(('rows', 'dict')), may hold values from 0 to 1
- decoding_table: bfloat16 [32768, 128], P('dict'), may hold values from -6 to 6
Outputs:
- compacted: bfloat16 [131072, 128], P(('rows', 'dict'))
The draws below stay inside these ranges and needn't reach their ends.
Inputs may be any that keep to these rules, and one draw needn't show every extreme that they name: Codes of the rows of one device lie in one range of 8192 consecutive lookup_keys_per_record (k * 8192 to (k + 1) * 8192 - 1) at most 1365 times, and exactly 1365 times for some range, whose rows all survive.
All inputs are finite; a program needn't handle non-finite values.
Results may differ from the reference program's by a relative error of at most 0.001.
Values may be sent and summed in bfloat16 or wider, within the bound.
A program may use at most 64 MiB of HBM per device.

```python
import jax
import jax.numpy as jnp

W = 128
VD = 8192
RD = 4096
CAP = 1365
VOCAB = 32768
ROWS_ALL = 131072


def joint_draw(key):
    blocks = ROWS_ALL // RD
    ranges = VOCAB // VD
    keys = jax.random.split(jax.random.fold_in(key, 11), 6)
    hot_range = jax.random.randint(keys[0], (blocks, 1), 0, ranges)
    row_orderings = jax.vmap(lambda k: jax.random.permutation(k, RD))(jax.random.split(keys[1], blocks))
    spread = (row_orderings - CAP) % (ranges - 1)
    others = (hot_range + 1 + spread) % ranges
    forced = row_orderings < CAP
    owner = jnp.where(forced, hot_range, others)
    first = jax.random.randint(keys[3], (blocks, RD), 0, VD)
    second = jax.random.randint(keys[4], (blocks, RD), 0, VD)
    inner = first * second // VD
    lookup_keys_per_record = (owner * VD + inner).reshape(ROWS_ALL).astype(jnp.int32)
    run_length = max(1, blocks // 8)
    run_count = (blocks + run_length - 1) // run_length
    run_levels = jax.random.randint(keys[2], (run_count,), 1, 20).astype(jnp.int32)
    run_of_block = (jnp.arange(blocks, dtype=jnp.int32) // run_length).astype(jnp.int32)
    levels = jnp.take(run_levels, run_of_block, axis=0)[:, None]
    drawn = jax.random.randint(keys[5], (blocks, RD), 0, 20)
    alive = forced | (drawn < levels)
    return (lookup_keys_per_record, alive.astype(jnp.int32).reshape(ROWS_ALL))


def draw_lookup_keys_per_record(key, part):
    return joint_draw(key)[0]


def draw_filter_passed_flags(key, part):
    return joint_draw(key)[1]


def block_levels(rng, dims, cuts, least, largest):
    loudness, own = 1.0, jax.random.fold_in(rng, 6)
    for dim, blocks in cuts:
        heights = jnp.exp(jax.random.uniform(jax.random.fold_in(own, dim), (blocks,), jnp.float32, least / len(cuts), largest / len(cuts)))
        loudness = loudness * jnp.repeat(heights, dims[dim] // blocks).reshape([-1 if axis == dim else 1 for axis in range(len(dims))])
    return loudness


def gaussian(key, shape, scale, reach, shards=(), kind=jnp.bfloat16):
    array = jax.random.normal(key, shape, jnp.float32) * scale
    if len(shards) > 0:
        array = block_levels(key, shape, shards, -0.22, 0.18) * array
    return jnp.clip(array, min=-reach, max=reach).astype(kind)


def setup_inputs(seed: int = 0) -> dict:
    splits = jax.random.split(jax.random.key(seed), 4)
    lookup_keys_per_record = draw_lookup_keys_per_record(jax.random.fold_in(splits[3], 71), 0)
    filter_passed_flags = draw_filter_passed_flags(jax.random.fold_in(splits[3], 71), 0)
    decoding_table = gaussian(splits[2], (VOCAB, W), 1.0, 6.0, ((0, 4),))
    return {"lookup_keys_per_record": lookup_keys_per_record, "filter_passed_flags": filter_passed_flags, "decoding_table": decoding_table}


def reference(lookup_keys_per_record, filter_passed_flags, decoding_table):
    keeper_flags = filter_passed_flags > 0
    overall_position = (jnp.cumsum(filter_passed_flags) - 1).astype(jnp.int32)
    decoded = jnp.take(decoding_table, lookup_keys_per_record, axis=0)
    target = jnp.where(keeper_flags, overall_position, jnp.int32(ROWS_ALL)).astype(jnp.int32)
    empty = jnp.zeros((ROWS_ALL, W), decoding_table.dtype)
    return empty.at[target].set(decoded, mode="drop")
```

```python
import functools

import jax
import jax.numpy as jnp
from jax import lax
from jax.experimental import pallas as pl
from jax.experimental.pallas import tpu as pltpu
from jax.sharding import PartitionSpec as P

LANES = 128


def shifted_left(x, step, lane):
    rows = x.shape[0]
    whole, rest = divmod(step, LANES)
    here = pltpu.roll(x, (rows - whole) % rows, 0) if whole % rows else x
    if rest == 0:
        return here
    above = pltpu.roll(here, rows - 1, 0) if rows > 1 else here
    return jnp.where(
        lane < LANES - rest,
        pltpu.roll(here, LANES - rest, 1),
        pltpu.roll(above, LANES - rest, 1),
    )


def running_sum(x, lane, row):
    rows = x.shape[0]
    total = x
    step = 1
    while step < LANES:
        total = total + jnp.where(lane >= step, pltpu.roll(total, step, 1), 0)
        step *= 2
    ends = jnp.broadcast_to(total[:, LANES - 1 :], x.shape)
    before = jnp.where(row >= 1, pltpu.roll(ends, 1, 0), 0)
    step = 1
    while step < rows:
        before = before + jnp.where(row >= step, pltpu.roll(before, step, 0), 0)
        step *= 2
    return total + before


def compact_kernel(codes_ref, flags_ref, out_ref):
    rows = codes_ref.shape[0]
    lane = lax.broadcasted_iota(jnp.int32, (rows, LANES), 1)
    row = lax.broadcasted_iota(jnp.int32, (rows, LANES), 0)
    kept = flags_ref[...] > 0
    sums = running_sum(kept.astype(jnp.int32), lane, row)
    position = row * LANES + lane
    tags = jnp.where(kept, position - sums + 2, 0)
    values = codes_ref[...]
    step = 1
    level = 0
    while step < rows * LANES:
        moving = (tags > 0) & (((tags - 1) >> level) & 1 == 1)
        arrived_tags = shifted_left(jnp.where(moving, tags, 0), step, lane)
        arrived_values = shifted_left(values, step, lane)
        arrives = (arrived_tags > 0) & (position < rows * LANES - step)
        values = jnp.where(arrives, arrived_values, values)
        tags = jnp.where(arrives, arrived_tags, jnp.where(moving, 0, tags))
        step *= 2
        level += 1
    out_ref[:rows, :] = values
    total = jnp.broadcast_to(sums[rows - 1 :, LANES - 1 :], (8, LANES))
    out_ref[rows:, :] = total


def pick_kernel(me_ref, counts_ref, codes_ref, out_ref):
    blocks = codes_ref.shape[0]
    rows = codes_ref.shape[1] - 8
    size = rows * LANES
    lane = lax.broadcasted_iota(jnp.int32, (rows, LANES), 1)
    row = lax.broadcasted_iota(jnp.int32, (rows, LANES), 0)
    position = row * LANES + lane
    out_ref[...] = jnp.full((rows, LANES), -1, jnp.int32)
    first = me_ref[0] * size

    def source(s, start):
        count = counts_ref[s]
        begin = start - first

        @pl.when((begin < size) & (begin + count > 0))
        def _():
            shift = lax.rem(begin + size, size)
            by_row = shift // LANES
            by_lane = lax.rem(shift, LANES)
            moved = pltpu.roll(codes_ref[s, :rows, :], by_row, 0)
            below = pltpu.roll(moved, 1, 0)
            picked = jnp.where(
                lane >= by_lane, pltpu.roll(moved, by_lane, 1), pltpu.roll(below, by_lane, 1)
            )
            inside = (position >= begin) & (position < begin + count)
            out_ref[...] = jnp.where(inside, picked, out_ref[...])

        return start + count

    lax.fori_loop(0, blocks, source, jnp.int32(0))


def on_device(lookup_keys_per_record, filter_passed_flags, decoding_table):
    rows_here = lookup_keys_per_record.shape[0]
    shard, width = decoding_table.shape
    groups = lax.axis_size("rows")
    rows = rows_here // LANES
    vmem = pl.BlockSpec(memory_space=pltpu.VMEM)
    smem = pl.BlockSpec(memory_space=pltpu.SMEM)

    part = shard // groups
    mine = lax.dynamic_slice_in_dim(decoding_table, lax.axis_index("rows") * part, part, 0)
    table = lax.all_gather(mine, ("dict", "rows"), tiled=True)

    compacted = pl.pallas_call(
        compact_kernel,
        out_shape=jax.ShapeDtypeStruct((rows + 8, LANES), jnp.int32),
        in_specs=[vmem, vmem],
        out_specs=vmem,
    )(lookup_keys_per_record.reshape(rows, LANES), filter_passed_flags.reshape(rows, LANES))
    everyone = lax.all_gather(compacted, ("rows", "dict"))
    counts = everyone[:, rows, 0]
    me = lax.axis_index(("rows", "dict")).astype(jnp.int32).reshape(1)
    codes = pl.pallas_call(
        pick_kernel,
        out_shape=jax.ShapeDtypeStruct((rows, LANES), jnp.int32),
        in_specs=[smem, smem, vmem],
        out_specs=vmem,
    )(me, counts, everyone).reshape(rows_here)
    picked = jnp.take(table, jnp.maximum(codes, 0), axis=0, mode="clip")
    return jnp.where((codes >= 0)[:, None], picked, jnp.zeros_like(picked))


def solution(mesh):
    placed = (P(("rows", "dict")), P(("rows", "dict")), P("dict", None))
    return jax.shard_map(
        on_device, mesh=mesh, in_specs=placed, out_specs=P(("rows", "dict"), None), check_vma=False
    )
```

```python
import functools

import jax
import jax.numpy as jnp
from jax import lax
from jax.experimental import pallas as pl
from jax.experimental.pallas import tpu as pltpu
from jax.sharding import PartitionSpec as P

LANES = 128


def shifted_left(x, step, lane):
    rows = x.shape[0]
    whole, rest = divmod(step, LANES)
    here = pltpu.roll(x, (rows - whole) % rows, 0) if whole % rows else x
    if rest == 0:
        return here
    above = pltpu.roll(here, rows - 1, 0) if rows > 1 else here
    return jnp.where(
        lane < LANES - rest,
        pltpu.roll(here, LANES - rest, 1),
        pltpu.roll(above, LANES - rest, 1),
    )


def running_sum(x, lane, row):
    rows = x.shape[0]
    total = x
    step = 1
    while step < LANES:
        total = total + jnp.where(lane >= step, pltpu.roll(total, step, 1), 0)
        step *= 2
    ends = jnp.broadcast_to(total[:, LANES - 1 :], x.shape)
    before = jnp.where(row >= 1, pltpu.roll(ends, 1, 0), 0)
    step = 1
    while step < rows:
        before = before + jnp.where(row >= step, pltpu.roll(before, step, 0), 0)
        step *= 2
    return total + before


def compact_kernel(codes_ref, flags_ref, out_ref):
    rows = codes_ref.shape[0]
    lane = lax.broadcasted_iota(jnp.int32, (rows, LANES), 1)
    row = lax.broadcasted_iota(jnp.int32, (rows, LANES), 0)
    kept = flags_ref[...] > 0
    sums = running_sum(kept.astype(jnp.int32), lane, row)
    position = row * LANES + lane
    tags = jnp.where(kept, position - sums + 2, 0)
    values = codes_ref[...]
    step = 1
    level = 0
    while step < rows * LANES:
        moving = (tags > 0) & (((tags - 1) >> level) & 1 == 1)
        arrived_tags = shifted_left(jnp.where(moving, tags, 0), step, lane)
        arrived_values = shifted_left(values, step, lane)
        arrives = (arrived_tags > 0) & (position < rows * LANES - step)
        values = jnp.where(arrives, arrived_values, values)
        tags = jnp.where(arrives, arrived_tags, jnp.where(moving, 0, tags))
        step *= 2
        level += 1
    out_ref[:rows, :] = values
    total = jnp.broadcast_to(sums[rows - 1 :, LANES - 1 :], (8, LANES))
    out_ref[rows:, :] = total


def pick_kernel(me_ref, counts_ref, codes_ref, out_ref):
    blocks = codes_ref.shape[0]
    rows = codes_ref.shape[1] - 8
    size = rows * LANES
    lane = lax.broadcasted_iota(jnp.int32, (rows, LANES), 1)
    row = lax.broadcasted_iota(jnp.int32, (rows, LANES), 0)
    position = row * LANES + lane
    out_ref[...] = jnp.full((rows, LANES), -1, jnp.int32)
    first = me_ref[0] * size

    def source(s, start):
        count = counts_ref[s]
        begin = start - first

        @pl.when((begin < size) & (begin + count > 0))
        def _():
            shift = lax.rem(begin + size, size)
            by_row = shift // LANES
            by_lane = lax.rem(shift, LANES)
            moved = pltpu.roll(codes_ref[s, :rows, :], by_row, 0)
            below = pltpu.roll(moved, 1, 0)
            picked = jnp.where(
                lane >= by_lane, pltpu.roll(moved, by_lane, 1), pltpu.roll(below, by_lane, 1)
            )
            inside = (position >= begin) & (position < begin + count)
            out_ref[...] = jnp.where(inside, picked, out_ref[...])

        return start + count

    lax.fori_loop(0, blocks, source, jnp.int32(0))


def forwarding(groups):
    bits = [1 << k for k in range(groups.bit_length() - 1)]
    return (bits[1:] + bits[:1], bits[:0:-1] + bits[:1])


def arrivals(order):
    arrived = [(0, -1)]
    for k, bit in enumerate(order):
        arrived += [(e ^ bit, k) for e, _ in arrived]
    return arrived


def table_kernel(groups, owners, shard_ref, out_ref, dict_send, dict_recv, send, recv, local):
    r = lax.axis_index("rows")
    z = lax.axis_index("dict")
    shard = shard_ref.shape[0]
    part = shard // groups
    half = part // 2
    orders = forwarding(groups)
    stages = [arrivals(order) for order in orders]

    def plane(peer):
        return {"rows": peer}

    def column(peer):
        return {"dict": peer}

    barrier = pltpu.get_barrier_semaphore()
    greeted = 0
    for d in range(1, owners):
        pl.semaphore_signal(
            barrier, inc=1, device_id=column(lax.rem(z + d, owners)), device_id_type=pl.DeviceIdType.MESH
        )
        greeted += 1
    for bit in orders[0]:
        pl.semaphore_signal(
            barrier, inc=1, device_id=plane(flipped(r, bit)), device_id_type=pl.DeviceIdType.MESH
        )
        greeted += 1
    pl.semaphore_wait(barrier, greeted)

    def place(owner, group, start, size):
        at = owner * shard + group * part + start
        return pl.ds(pl.multiple_of(at, half), size)

    nearest = sorted(range(1, owners), key=lambda d: min(d, owners - d))
    sent = []
    for d in nearest:
        copy = pltpu.make_async_remote_copy(
            src_ref=shard_ref.at[pl.ds(pl.multiple_of(r * part, part), part)],
            dst_ref=out_ref.at[place(z, r, 0, part)],
            send_sem=dict_send.at[d - 1],
            recv_sem=dict_recv.at[d - 1],
            device_id=column(lax.rem(z + d, owners)),
            device_id_type=pl.DeviceIdType.MESH,
        )
        copy.start()
        sent.append(copy)
    own = pltpu.make_async_copy(
        shard_ref, out_ref.at[pl.ds(pl.multiple_of(z * shard, shard), shard)], local.at[0]
    )
    own.start()

    received = {}
    first = {d: sent[i] for i, d in enumerate(nearest)}
    for index in range(groups):
        for d in nearest:
            owner = lax.rem(z + owners - d, owners)
            if index == 0:
                first[d].wait_recv()
            for h in range(2):
                offset, k = stages[h][index]
                if index > 0:
                    received[d, h, offset].wait_recv()
                where = place(owner, flipped(r, offset), h * half, half)
                for later in range(k + 1, len(orders[h])):
                    bit = orders[h][later]
                    lane = ((d - 1) * 2 + h) * groups + (offset ^ bit)
                    copy = pltpu.make_async_remote_copy(
                        src_ref=out_ref.at[where],
                        dst_ref=out_ref.at[where],
                        send_sem=send.at[lane],
                        recv_sem=recv.at[lane],
                        device_id=plane(flipped(r, bit)),
                        device_id_type=pl.DeviceIdType.MESH,
                    )
                    copy.start()
                    sent.append(copy)
                    received[d, h, offset ^ bit] = copy
    for copy in sent:
        copy.wait_send()
    own.wait()


def flipped(r, mask):
    out = r
    bit = 1
    while bit <= mask:
        if mask & bit:
            out = out + bit - 2 * bit * lax.rem(lax.div(r, bit), 2)
        bit *= 2
    return out


def gathered_table(decoding_table):
    groups = lax.axis_size("rows")
    owners = lax.axis_size("dict")
    shard, width = decoding_table.shape
    flights = (owners - 1) * 2 * groups
    return pl.pallas_call(
        functools.partial(table_kernel, groups, owners),
        out_shape=jax.ShapeDtypeStruct((owners * shard, width), decoding_table.dtype),
        in_specs=[pl.BlockSpec(memory_space=pltpu.VMEM)],
        out_specs=pl.BlockSpec(memory_space=pl.ANY),
        scratch_shapes=[
            pltpu.SemaphoreType.DMA((owners - 1,)),
            pltpu.SemaphoreType.DMA((owners - 1,)),
            pltpu.SemaphoreType.DMA((flights,)),
            pltpu.SemaphoreType.DMA((flights,)),
            pltpu.SemaphoreType.DMA((1,)),
        ],
        compiler_params=pltpu.CompilerParams(collective_id=0, has_side_effects=True),
        cost_estimate=pl.CostEstimate(
            flops=0, bytes_accessed=16 * owners * shard * width, transcendentals=0
        ),
    )(decoding_table)


def on_device(lookup_keys_per_record, filter_passed_flags, decoding_table):
    rows_here = lookup_keys_per_record.shape[0]
    shard, width = decoding_table.shape
    rows = rows_here // LANES
    vmem = pl.BlockSpec(memory_space=pltpu.VMEM)
    smem = pl.BlockSpec(memory_space=pltpu.SMEM)

    table = gathered_table(decoding_table)

    compacted = pl.pallas_call(
        compact_kernel,
        out_shape=jax.ShapeDtypeStruct((rows + 8, LANES), jnp.int32),
        in_specs=[vmem, vmem],
        out_specs=vmem,
    )(lookup_keys_per_record.reshape(rows, LANES), filter_passed_flags.reshape(rows, LANES))
    everyone = lax.all_gather(compacted, ("rows", "dict"))
    counts = everyone[:, rows, 0]
    me = lax.axis_index(("rows", "dict")).astype(jnp.int32).reshape(1)
    codes = pl.pallas_call(
        pick_kernel,
        out_shape=jax.ShapeDtypeStruct((rows, LANES), jnp.int32),
        in_specs=[smem, smem, vmem],
        out_specs=vmem,
    )(me, counts, everyone).reshape(rows_here)
    picked = jnp.take(table, jnp.maximum(codes, 0), axis=0, mode="clip")
    return jnp.where((codes >= 0)[:, None], picked, jnp.zeros_like(picked))


def solution(mesh):
    placed = (P(("rows", "dict")), P(("rows", "dict")), P("dict", None))
    return jax.shard_map(
        on_device, mesh=mesh, in_specs=placed, out_specs=P(("rows", "dict"), None), check_vma=False
    )
```

```python
import functools

import jax
import jax.numpy as jnp
from jax import lax
from jax.experimental import pallas as pl
from jax.experimental.pallas import tpu as pltpu
from jax.sharding import PartitionSpec as P

LANES = 128


def shifted_left(x, step, lane):
    rows = x.shape[0]
    whole, rest = divmod(step, LANES)
    here = pltpu.roll(x, (rows - whole) % rows, 0) if whole % rows else x
    if rest == 0:
        return here
    above = pltpu.roll(here, rows - 1, 0) if rows > 1 else here
    return jnp.where(
        lane < LANES - rest,
        pltpu.roll(here, LANES - rest, 1),
        pltpu.roll(above, LANES - rest, 1),
    )


def running_sum(x, lane, row):
    rows = x.shape[0]
    total = x
    step = 1
    while step < LANES:
        total = total + jnp.where(lane >= step, pltpu.roll(total, step, 1), 0)
        step *= 2
    ends = jnp.broadcast_to(total[:, LANES - 1 :], x.shape)
    before = jnp.where(row >= 1, pltpu.roll(ends, 1, 0), 0)
    step = 1
    while step < rows:
        before = before + jnp.where(row >= step, pltpu.roll(before, step, 0), 0)
        step *= 2
    return total + before


def compact_kernel(codes_ref, flags_ref, out_ref):
    rows = codes_ref.shape[0]
    lane = lax.broadcasted_iota(jnp.int32, (rows, LANES), 1)
    row = lax.broadcasted_iota(jnp.int32, (rows, LANES), 0)
    kept = flags_ref[...] > 0
    sums = running_sum(kept.astype(jnp.int32), lane, row)
    position = row * LANES + lane
    tags = jnp.where(kept, position - sums + 2, 0)
    values = codes_ref[...]
    step = 1
    level = 0
    while step < rows * LANES:
        moving = (tags > 0) & (((tags - 1) >> level) & 1 == 1)
        arrived_tags = shifted_left(jnp.where(moving, tags, 0), step, lane)
        arrived_values = shifted_left(values, step, lane)
        arrives = (arrived_tags > 0) & (position < rows * LANES - step)
        values = jnp.where(arrives, arrived_values, values)
        tags = jnp.where(arrives, arrived_tags, jnp.where(moving, 0, tags))
        step *= 2
        level += 1
    out_ref[:rows, :] = values
    total = jnp.broadcast_to(sums[rows - 1 :, LANES - 1 :], (8, LANES))
    out_ref[rows:, :] = total


def pick_kernel(blank, me_ref, counts_ref, codes_ref, out_ref):
    blocks = codes_ref.shape[0]
    rows = codes_ref.shape[1] - 8
    size = rows * LANES
    lane = lax.broadcasted_iota(jnp.int32, (rows, LANES), 1)
    row = lax.broadcasted_iota(jnp.int32, (rows, LANES), 0)
    position = row * LANES + lane
    out_ref[...] = jnp.full((rows, LANES), blank, jnp.int32)
    first = me_ref[0] * size

    def source(s, start):
        count = counts_ref[s]
        begin = start - first

        @pl.when((begin < size) & (begin + count > 0))
        def _():
            shift = lax.rem(begin + size, size)
            by_row = shift // LANES
            by_lane = lax.rem(shift, LANES)
            moved = pltpu.roll(codes_ref[s, :rows, :], by_row, 0)
            below = pltpu.roll(moved, 1, 0)
            picked = jnp.where(
                lane >= by_lane, pltpu.roll(moved, by_lane, 1), pltpu.roll(below, by_lane, 1)
            )
            inside = (position >= begin) & (position < begin + count)
            out_ref[...] = jnp.where(inside, picked, out_ref[...])

        return start + count

    lax.fori_loop(0, blocks, source, jnp.int32(0))


def forwarding(groups):
    bits = [1 << k for k in range(groups.bit_length() - 1)]
    return (bits[1:] + bits[:1], bits[:0:-1] + bits[:1])


def arrivals(order):
    arrived = [(0, -1)]
    for k, bit in enumerate(order):
        arrived += [(e ^ bit, k) for e, _ in arrived]
    return arrived


def table_kernel(
    groups,
    owners,
    shard_ref,
    zeros_ref,
    codes_ref,
    out_ref,
    everyone_ref,
    dict_send,
    dict_recv,
    send,
    recv,
    code_dict_send,
    code_dict_recv,
    code_send,
    code_recv,
    local,
):
    r = lax.axis_index("rows")
    z = lax.axis_index("dict")
    shard = shard_ref.shape[0]
    part = shard // groups
    half = part // 2
    orders = forwarding(groups)
    stages = [arrivals(order) for order in orders]

    def plane(peer):
        return {"rows": peer}

    def column(peer):
        return {"dict": peer}

    barrier = pltpu.get_barrier_semaphore()
    greeted = 0
    for d in range(1, owners):
        pl.semaphore_signal(
            barrier, inc=1, device_id=column(lax.rem(z + d, owners)), device_id_type=pl.DeviceIdType.MESH
        )
        greeted += 1
    for bit in orders[0]:
        pl.semaphore_signal(
            barrier, inc=1, device_id=plane(flipped(r, bit)), device_id_type=pl.DeviceIdType.MESH
        )
        greeted += 1
    pl.semaphore_wait(barrier, greeted)

    def place(owner, group, start, size):
        at = owner * shard + group * part + start
        return pl.ds(pl.multiple_of(at, half), size)

    nearest = sorted(range(1, owners), key=lambda d: min(d, owners - d))
    sent = []

    def to(src, dst, send_sem, recv_sem, peer):
        copy = pltpu.make_async_remote_copy(
            src_ref=src,
            dst_ref=dst,
            send_sem=send_sem,
            recv_sem=recv_sem,
            device_id=peer,
            device_id_type=pl.DeviceIdType.MESH,
        )
        copy.start()
        sent.append(copy)
        return copy

    first = {}
    mine = everyone_ref.at[r * owners + z]
    code_first = {}
    code_received = {}
    code_order = orders[0]
    code_stages = stages[0]

    def forward_codes(src, d, offset, k):
        owner = lax.rem(z + owners - d, owners)
        dst = everyone_ref.at[flipped(r, offset) * owners + owner]
        for later in range(k + 1, len(code_order)):
            bit = code_order[later]
            lane = d * groups + (offset ^ bit)
            code_received[d, offset ^ bit] = to(
                dst if src is None else src,
                dst,
                code_send.at[lane],
                code_recv.at[lane],
                plane(flipped(r, bit)),
            )

    for d in nearest:
        code_first[d] = to(
            codes_ref,
            mine,
            code_dict_send.at[d - 1],
            code_dict_recv.at[d - 1],
            column(lax.rem(z + d, owners)),
        )
    forward_codes(codes_ref, 0, 0, -1)
    for d in nearest:
        copy = pltpu.make_async_remote_copy(
            src_ref=shard_ref.at[pl.ds(pl.multiple_of(r * part, part), part)],
            dst_ref=out_ref.at[place(z, r, 0, part)],
            send_sem=dict_send.at[d - 1],
            recv_sem=dict_recv.at[d - 1],
            device_id=column(lax.rem(z + d, owners)),
            device_id_type=pl.DeviceIdType.MESH,
        )
        copy.start()
        sent.append(copy)
        first[d] = copy
    own = pltpu.make_async_copy(
        shard_ref, out_ref.at[pl.ds(pl.multiple_of(z * shard, shard), shard)], local.at[0]
    )
    own.start()
    blank = pltpu.make_async_copy(
        zeros_ref, out_ref.at[pl.ds(owners * shard, zeros_ref.shape[0])], local.at[1]
    )
    blank.start()
    own_codes = pltpu.make_async_copy(codes_ref, mine, local.at[2])
    own_codes.start()

    received = {}
    for index, (offset, k) in enumerate(code_stages):
        for d in [0] + nearest:
            if index == 0:
                if d == 0:
                    continue
                code_first[d].wait_recv()
            else:
                code_received[d, offset].wait_recv()
            forward_codes(None, d, offset, k)
    for index in range(groups):
        for d in nearest:
            owner = lax.rem(z + owners - d, owners)
            if index == 0:
                first[d].wait_recv()
            for h in range(2):
                offset, k = stages[h][index]
                if index > 0:
                    received[d, h, offset].wait_recv()
                where = place(owner, flipped(r, offset), h * half, half)
                for later in range(k + 1, len(orders[h])):
                    bit = orders[h][later]
                    lane = ((d - 1) * 2 + h) * groups + (offset ^ bit)
                    copy = pltpu.make_async_remote_copy(
                        src_ref=out_ref.at[where],
                        dst_ref=out_ref.at[where],
                        send_sem=send.at[lane],
                        recv_sem=recv.at[lane],
                        device_id=plane(flipped(r, bit)),
                        device_id_type=pl.DeviceIdType.MESH,
                    )
                    copy.start()
                    sent.append(copy)
                    received[d, h, offset ^ bit] = copy
    for copy in sent:
        copy.wait_send()
    own.wait()
    blank.wait()
    own_codes.wait()


def flipped(r, mask):
    out = r
    bit = 1
    while bit <= mask:
        if mask & bit:
            out = out + bit - 2 * bit * lax.rem(lax.div(r, bit), 2)
        bit *= 2
    return out


def gathered(decoding_table, compacted):
    groups = lax.axis_size("rows")
    owners = lax.axis_size("dict")
    shard, width = decoding_table.shape
    flights = (owners - 1) * 2 * groups
    vmem = pl.BlockSpec(memory_space=pltpu.VMEM)
    anywhere = pl.BlockSpec(memory_space=pl.ANY)
    zeros = jnp.zeros((16, width), decoding_table.dtype)
    return pl.pallas_call(
        functools.partial(table_kernel, groups, owners),
        out_shape=(
            jax.ShapeDtypeStruct((owners * shard + 16, width), decoding_table.dtype),
            jax.ShapeDtypeStruct((owners * groups,) + compacted.shape, compacted.dtype),
        ),
        in_specs=[vmem, vmem, vmem],
        out_specs=(anywhere, anywhere),
        scratch_shapes=[
            pltpu.SemaphoreType.DMA((owners - 1,)),
            pltpu.SemaphoreType.DMA((owners - 1,)),
            pltpu.SemaphoreType.DMA((flights,)),
            pltpu.SemaphoreType.DMA((flights,)),
            pltpu.SemaphoreType.DMA((owners - 1,)),
            pltpu.SemaphoreType.DMA((owners - 1,)),
            pltpu.SemaphoreType.DMA((owners * groups,)),
            pltpu.SemaphoreType.DMA((owners * groups,)),
            pltpu.SemaphoreType.DMA((3,)),
        ],
        compiler_params=pltpu.CompilerParams(collective_id=0, has_side_effects=True),
        cost_estimate=pl.CostEstimate(
            flops=0, bytes_accessed=16 * owners * shard * width, transcendentals=0
        ),
    )(decoding_table, zeros, compacted)


def on_device(lookup_keys_per_record, filter_passed_flags, decoding_table):
    rows_here = lookup_keys_per_record.shape[0]
    shard, width = decoding_table.shape
    rows = rows_here // LANES
    vmem = pl.BlockSpec(memory_space=pltpu.VMEM)
    smem = pl.BlockSpec(memory_space=pltpu.SMEM)

    compacted = pl.pallas_call(
        compact_kernel,
        out_shape=jax.ShapeDtypeStruct((rows + 8, LANES), jnp.int32),
        in_specs=[vmem, vmem],
        out_specs=vmem,
    )(lookup_keys_per_record.reshape(rows, LANES), filter_passed_flags.reshape(rows, LANES))
    table, everyone = gathered(decoding_table, compacted)
    counts = everyone[:, rows, 0]
    me = lax.axis_index(("rows", "dict")).astype(jnp.int32).reshape(1)
    codes = pl.pallas_call(
        functools.partial(pick_kernel, shard * lax.axis_size("dict")),
        out_shape=jax.ShapeDtypeStruct((rows, LANES), jnp.int32),
        in_specs=[smem, smem, vmem],
        out_specs=vmem,
    )(me, counts, everyone).reshape(rows_here)
    return table.at[codes].get(mode="promise_in_bounds")


def solution(mesh):
    placed = (P(("rows", "dict")), P(("rows", "dict")), P("dict", None))
    return jax.shard_map(
        on_device, mesh=mesh, in_specs=placed, out_specs=P(("rows", "dict"), None), check_vma=False
    )
```

```python
import functools

import jax
import jax.numpy as jnp
from jax import lax
from jax.experimental import pallas as pl
from jax.experimental.pallas import tpu as pltpu
from jax.sharding import PartitionSpec as P

LANES = 128
GRANT = 12 * 1024 * 1024


def shifted_left(x, step, lane):
    rows = x.shape[0]
    whole, rest = divmod(step, LANES)
    here = pltpu.roll(x, (rows - whole) % rows, 0) if whole % rows else x
    if rest == 0:
        return here
    above = pltpu.roll(here, rows - 1, 0) if rows > 1 else here
    return jnp.where(
        lane < LANES - rest,
        pltpu.roll(here, LANES - rest, 1),
        pltpu.roll(above, LANES - rest, 1),
    )


def running_sum(x, lane, row):
    rows = x.shape[0]
    total = x
    step = 1
    while step < LANES:
        total = total + jnp.where(lane >= step, pltpu.roll(total, step, 1), 0)
        step *= 2
    ends = jnp.broadcast_to(total[:, LANES - 1 :], x.shape)
    before = jnp.where(row >= 1, pltpu.roll(ends, 1, 0), 0)
    step = 1
    while step < rows:
        before = before + jnp.where(row >= step, pltpu.roll(before, step, 0), 0)
        step *= 2
    return total + before


def compact_kernel(codes_ref, flags_ref, out_ref):
    rows = codes_ref.shape[0]
    lane = lax.broadcasted_iota(jnp.int32, (rows, LANES), 1)
    row = lax.broadcasted_iota(jnp.int32, (rows, LANES), 0)
    kept = flags_ref[...] > 0
    sums = running_sum(kept.astype(jnp.int32), lane, row)
    position = row * LANES + lane
    tags = jnp.where(kept, position - sums + 2, 0)
    values = codes_ref[...]
    step = 1
    level = 0
    while step < rows * LANES:
        moving = (tags > 0) & (((tags - 1) >> level) & 1 == 1)
        arrived_tags = shifted_left(jnp.where(moving, tags, 0), step, lane)
        arrived_values = shifted_left(values, step, lane)
        arrives = (arrived_tags > 0) & (position < rows * LANES - step)
        values = jnp.where(arrives, arrived_values, values)
        tags = jnp.where(arrives, arrived_tags, jnp.where(moving, 0, tags))
        step *= 2
        level += 1
    out_ref[:rows, :] = values
    total = jnp.broadcast_to(sums[rows - 1 :, LANES - 1 :], (8, LANES))
    out_ref[rows:, :] = total


def decode_kernel(
    blank, me_ref, codes_ref, table_ref, out_ref, picked, tallies, rows_f32, counts, codes, sem
):
    blocks = codes_ref.shape[0]
    rows = codes_ref.shape[1] - 8
    size = rows * LANES
    lane = lax.broadcasted_iota(jnp.int32, (rows, LANES), 1)
    row = lax.broadcasted_iota(jnp.int32, (rows, LANES), 0)
    position = row * LANES + lane
    tallies[...] = codes_ref[:, rows, :]
    copy = pltpu.make_async_copy(tallies, counts, sem.at[0])
    copy.start()
    picked[...] = jnp.full((rows, LANES), blank, jnp.int32)
    first = me_ref[0] * size
    copy.wait()

    def source(s, start):
        count = counts[s, 0]
        begin = start - first

        @pl.when((begin < size) & (begin + count > 0))
        def _():
            shift = lax.rem(begin + size, size)
            by_row = shift // LANES
            by_lane = lax.rem(shift, LANES)
            moved = pltpu.roll(codes_ref[s, :rows, :], by_row, 0)
            below = pltpu.roll(moved, 1, 0)
            mine = jnp.where(
                lane >= by_lane, pltpu.roll(moved, by_lane, 1), pltpu.roll(below, by_lane, 1)
            )
            inside = (position >= begin) & (position < begin + count)
            picked[...] = jnp.where(inside, mine, picked[...])

        return start + count

    lax.fori_loop(0, blocks, source, jnp.int32(0))
    copy = pltpu.make_async_copy(picked, codes, sem.at[1])
    copy.start()
    copy.wait()

    @pl.loop(0, rows)
    def _(i):
        for j in range(LANES):
            code = codes[i, j]
            pair = table_ref[code >> 1].astype(jnp.float32)
            odd = (code & 1) == 1
            rows_f32[pl.ds(i * LANES + j, 1), :] = jnp.where(odd, pair[1:2], pair[0:1])

    @pl.loop(0, rows)
    def _(i):
        block = pl.ds(pl.multiple_of(i * LANES, LANES), LANES)
        out_ref[block, :] = rows_f32[block, :].astype(out_ref.dtype)


def forwarding(groups):
    bits = [1 << k for k in range(groups.bit_length() - 1)]
    return (bits[1:] + bits[:1], bits[:0:-1] + bits[:1])


def arrivals(order):
    arrived = [(0, -1)]
    for k, bit in enumerate(order):
        arrived += [(e ^ bit, k) for e, _ in arrived]
    return arrived


def table_kernel(
    groups,
    owners,
    shard_ref,
    zeros_ref,
    codes_ref,
    out_ref,
    everyone_ref,
    dict_send,
    dict_recv,
    send,
    recv,
    code_dict_send,
    code_dict_recv,
    code_send,
    code_recv,
    local,
):
    r = lax.axis_index("rows")
    z = lax.axis_index("dict")
    shard = shard_ref.shape[0]
    part = shard // groups
    half = part // 2
    orders = forwarding(groups)
    stages = [arrivals(order) for order in orders]

    def plane(peer):
        return {"rows": peer}

    def column(peer):
        return {"dict": peer}

    barrier = pltpu.get_barrier_semaphore()
    greeted = 0
    for d in range(1, owners):
        pl.semaphore_signal(
            barrier, inc=1, device_id=column(lax.rem(z + d, owners)), device_id_type=pl.DeviceIdType.MESH
        )
        greeted += 1
    for bit in orders[0]:
        pl.semaphore_signal(
            barrier, inc=1, device_id=plane(flipped(r, bit)), device_id_type=pl.DeviceIdType.MESH
        )
        greeted += 1
    pl.semaphore_wait(barrier, greeted)

    def place(owner, group, start, size):
        at = owner * shard + group * part + start
        return pl.ds(pl.multiple_of(at, half), size)

    nearest = sorted(range(1, owners), key=lambda d: min(d, owners - d))
    sent = []

    def to(src, dst, send_sem, recv_sem, peer):
        copy = pltpu.make_async_remote_copy(
            src_ref=src,
            dst_ref=dst,
            send_sem=send_sem,
            recv_sem=recv_sem,
            device_id=peer,
            device_id_type=pl.DeviceIdType.MESH,
        )
        copy.start()
        sent.append(copy)
        return copy

    first = {}
    mine = everyone_ref.at[r * owners + z]
    code_first = {}
    code_received = {}
    code_order = orders[0]
    code_stages = stages[0]

    def forward_codes(src, d, offset, k):
        owner = lax.rem(z + owners - d, owners)
        dst = everyone_ref.at[flipped(r, offset) * owners + owner]
        for later in range(k + 1, len(code_order)):
            bit = code_order[later]
            lane = d * groups + (offset ^ bit)
            code_received[d, offset ^ bit] = to(
                dst if src is None else src,
                dst,
                code_send.at[lane],
                code_recv.at[lane],
                plane(flipped(r, bit)),
            )

    for d in nearest:
        code_first[d] = to(
            codes_ref,
            mine,
            code_dict_send.at[d - 1],
            code_dict_recv.at[d - 1],
            column(lax.rem(z + d, owners)),
        )
    forward_codes(codes_ref, 0, 0, -1)
    for d in nearest:
        copy = pltpu.make_async_remote_copy(
            src_ref=shard_ref.at[pl.ds(pl.multiple_of(r * part, part), part)],
            dst_ref=out_ref.at[place(z, r, 0, part)],
            send_sem=dict_send.at[d - 1],
            recv_sem=dict_recv.at[d - 1],
            device_id=column(lax.rem(z + d, owners)),
            device_id_type=pl.DeviceIdType.MESH,
        )
        copy.start()
        sent.append(copy)
        first[d] = copy
    own = pltpu.make_async_copy(
        shard_ref, out_ref.at[pl.ds(pl.multiple_of(z * shard, shard), shard)], local.at[0]
    )
    own.start()
    blank = pltpu.make_async_copy(
        zeros_ref, out_ref.at[pl.ds(owners * shard, zeros_ref.shape[0])], local.at[1]
    )
    blank.start()
    own_codes = pltpu.make_async_copy(codes_ref, mine, local.at[2])
    own_codes.start()

    received = {}
    for index in range(groups):
        for d in nearest:
            owner = lax.rem(z + owners - d, owners)
            if index == 0:
                first[d].wait_recv()
            for h in range(2):
                offset, k = stages[h][index]
                if index > 0:
                    received[d, h, offset].wait_recv()
                where = place(owner, flipped(r, offset), h * half, half)
                for later in range(k + 1, len(orders[h])):
                    bit = orders[h][later]
                    lane = ((d - 1) * 2 + h) * groups + (offset ^ bit)
                    copy = pltpu.make_async_remote_copy(
                        src_ref=out_ref.at[where],
                        dst_ref=out_ref.at[where],
                        send_sem=send.at[lane],
                        recv_sem=recv.at[lane],
                        device_id=plane(flipped(r, bit)),
                        device_id_type=pl.DeviceIdType.MESH,
                    )
                    copy.start()
                    sent.append(copy)
                    received[d, h, offset ^ bit] = copy
        offset, k = code_stages[index]
        for d in [0] + nearest:
            if index == 0:
                if d == 0:
                    continue
                code_first[d].wait_recv()
            else:
                code_received[d, offset].wait_recv()
            forward_codes(None, d, offset, k)
    for copy in sent:
        copy.wait_send()
    own.wait()
    blank.wait()
    own_codes.wait()


def flipped(r, mask):
    out = r
    bit = 1
    while bit <= mask:
        if mask & bit:
            out = out + bit - 2 * bit * lax.rem(lax.div(r, bit), 2)
        bit *= 2
    return out


def gathered(decoding_table, compacted):
    groups = lax.axis_size("rows")
    owners = lax.axis_size("dict")
    shard, width = decoding_table.shape
    flights = (owners - 1) * 2 * groups
    vmem = pl.BlockSpec(memory_space=pltpu.VMEM)
    anywhere = pl.BlockSpec(memory_space=pl.ANY)
    zeros = jnp.zeros((16, width), decoding_table.dtype)
    return pl.pallas_call(
        functools.partial(table_kernel, groups, owners),
        out_shape=(
            jax.ShapeDtypeStruct((owners * shard + 16, width), decoding_table.dtype),
            jax.ShapeDtypeStruct((owners * groups,) + compacted.shape, compacted.dtype),
        ),
        in_specs=[vmem, vmem, vmem],
        out_specs=(anywhere, anywhere),
        scratch_shapes=[
            pltpu.SemaphoreType.DMA((owners - 1,)),
            pltpu.SemaphoreType.DMA((owners - 1,)),
            pltpu.SemaphoreType.DMA((flights,)),
            pltpu.SemaphoreType.DMA((flights,)),
            pltpu.SemaphoreType.DMA((owners - 1,)),
            pltpu.SemaphoreType.DMA((owners - 1,)),
            pltpu.SemaphoreType.DMA((owners * groups,)),
            pltpu.SemaphoreType.DMA((owners * groups,)),
            pltpu.SemaphoreType.DMA((3,)),
        ],
        compiler_params=pltpu.CompilerParams(
            collective_id=0, has_side_effects=True, vmem_limit_bytes=GRANT
        ),
        cost_estimate=pl.CostEstimate(
            flops=0, bytes_accessed=16 * owners * shard * width, transcendentals=0
        ),
    )(decoding_table, zeros, compacted)


def on_device(lookup_keys_per_record, filter_passed_flags, decoding_table):
    rows_here = lookup_keys_per_record.shape[0]
    shard, width = decoding_table.shape
    rows = rows_here // LANES
    vmem = pl.BlockSpec(memory_space=pltpu.VMEM)
    smem = pl.BlockSpec(memory_space=pltpu.SMEM)

    compacted = pl.pallas_call(
        compact_kernel,
        out_shape=jax.ShapeDtypeStruct((rows + 8, LANES), jnp.int32),
        in_specs=[vmem, vmem],
        out_specs=vmem,
        compiler_params=pltpu.CompilerParams(vmem_limit_bytes=GRANT),
    )(lookup_keys_per_record.reshape(rows, LANES), filter_passed_flags.reshape(rows, LANES))
    table, everyone = gathered(decoding_table, compacted)
    me = lax.axis_index(("rows", "dict")).astype(jnp.int32).reshape(1)
    blank = shard * lax.axis_size("dict")
    blocks = everyone.shape[0]
    return pl.pallas_call(
        functools.partial(decode_kernel, blank),
        out_shape=jax.ShapeDtypeStruct((rows_here, width), decoding_table.dtype),
        in_specs=[smem, vmem, vmem],
        out_specs=vmem,
        scratch_shapes=[
            pltpu.VMEM((rows, LANES), jnp.int32),
            pltpu.VMEM((blocks, LANES), jnp.int32),
            pltpu.VMEM((rows_here, width), jnp.float32),
            pltpu.SMEM((blocks, LANES), jnp.int32),
            pltpu.SMEM((rows, LANES), jnp.int32),
            pltpu.SemaphoreType.DMA((2,)),
        ],
        compiler_params=pltpu.CompilerParams(vmem_limit_bytes=40 * 1024 * 1024),
    )(me, everyone, table.reshape(table.shape[0] // 2, 2, width))


def solution(mesh):
    placed = (P(("rows", "dict")), P(("rows", "dict")), P("dict", None))
    return jax.shard_map(
        on_device, mesh=mesh, in_specs=placed, out_specs=P(("rows", "dict"), None), check_vma=False
    )
```

```python
import functools

import jax
import jax.numpy as jnp
from jax import lax
from jax.experimental import pallas as pl
from jax.experimental.pallas import tpu as pltpu
from jax.sharding import PartitionSpec as P

LANES = 128
GRANT = 12 * 1024 * 1024


def shifted_left(x, step, lane):
    rows = x.shape[0]
    whole, rest = divmod(step, LANES)
    here = pltpu.roll(x, (rows - whole) % rows, 0) if whole % rows else x
    if rest == 0:
        return here
    above = pltpu.roll(here, rows - 1, 0) if rows > 1 else here
    return jnp.where(
        lane < LANES - rest,
        pltpu.roll(here, LANES - rest, 1),
        pltpu.roll(above, LANES - rest, 1),
    )


def running_sum(x, lane, row):
    rows = x.shape[0]
    total = x
    step = 1
    while step < LANES:
        total = total + jnp.where(lane >= step, pltpu.roll(total, step, 1), 0)
        step *= 2
    ends = jnp.broadcast_to(total[:, LANES - 1 :], x.shape)
    before = jnp.where(row >= 1, pltpu.roll(ends, 1, 0), 0)
    step = 1
    while step < rows:
        before = before + jnp.where(row >= step, pltpu.roll(before, step, 0), 0)
        step *= 2
    return total + before


def compact_kernel(codes_ref, flags_ref, out_ref):
    rows = codes_ref.shape[0]
    lane = lax.broadcasted_iota(jnp.int32, (rows, LANES), 1)
    row = lax.broadcasted_iota(jnp.int32, (rows, LANES), 0)
    kept = flags_ref[...] > 0
    sums = running_sum(kept.astype(jnp.int32), lane, row)
    position = row * LANES + lane
    tags = jnp.where(kept, position - sums + 2, 0)
    values = codes_ref[...]
    step = 1
    level = 0
    while step < rows * LANES:
        moving = (tags > 0) & (((tags - 1) >> level) & 1 == 1)
        arrived_tags = shifted_left(jnp.where(moving, tags, 0), step, lane)
        arrived_values = shifted_left(values, step, lane)
        arrives = (arrived_tags > 0) & (position < rows * LANES - step)
        values = jnp.where(arrives, arrived_values, values)
        tags = jnp.where(arrives, arrived_tags, jnp.where(moving, 0, tags))
        step *= 2
        level += 1
    out_ref[:rows, :] = values
    total = jnp.broadcast_to(sums[rows - 1 :, LANES - 1 :], (8, LANES))
    out_ref[rows:, :] = total


def decode_kernel(
    blank, me_ref, codes_ref, table_ref, out_ref, picked, tallies, rows_f32, counts, codes, sem
):
    blocks = codes_ref.shape[0]
    rows = codes_ref.shape[1] - 8
    size = rows * LANES
    lane = lax.broadcasted_iota(jnp.int32, (rows, LANES), 1)
    row = lax.broadcasted_iota(jnp.int32, (rows, LANES), 0)
    position = row * LANES + lane
    tallies[...] = codes_ref[:, rows, :]
    copy = pltpu.make_async_copy(tallies, counts, sem.at[0])
    copy.start()
    picked[...] = jnp.full((rows, LANES), blank, jnp.int32)
    first = me_ref[0] * size
    copy.wait()

    def source(s, start):
        count = counts[s, 0]
        begin = start - first

        @pl.when((begin < size) & (begin + count > 0))
        def _():
            shift = lax.rem(begin + size, size)
            by_row = shift // LANES
            by_lane = lax.rem(shift, LANES)
            moved = pltpu.roll(codes_ref[s, :rows, :], by_row, 0)
            below = pltpu.roll(moved, 1, 0)
            mine = jnp.where(
                lane >= by_lane, pltpu.roll(moved, by_lane, 1), pltpu.roll(below, by_lane, 1)
            )
            inside = (position >= begin) & (position < begin + count)
            picked[...] = jnp.where(inside, mine, picked[...])

        return start + count

    lax.fori_loop(0, blocks, source, jnp.int32(0))
    copy = pltpu.make_async_copy(picked, codes, sem.at[1])
    copy.start()
    copy.wait()

    @pl.loop(0, rows)
    def _(i):
        for j in range(LANES):
            code = codes[i, j]
            pair = table_ref[code >> 1].astype(jnp.float32)
            odd = (code & 1) == 1
            rows_f32[pl.ds(i * LANES + j, 1), :] = jnp.where(odd, pair[1:2], pair[0:1])

    @pl.loop(0, rows)
    def _(i):
        block = pl.ds(pl.multiple_of(i * LANES, LANES), LANES)
        out_ref[block, :] = rows_f32[block, :].astype(out_ref.dtype)


def forwarding(groups):
    bits = [1 << k for k in range(groups.bit_length() - 1)]
    return (bits[1:] + bits[:1], bits[:0:-1] + bits[:1])


def arrivals(order):
    arrived = [(0, -1)]
    for k, bit in enumerate(order):
        arrived += [(e ^ bit, k) for e, _ in arrived]
    return arrived


def table_kernel(
    groups,
    owners,
    shard_ref,
    zeros_ref,
    codes_ref,
    out_ref,
    everyone_ref,
    dict_send,
    dict_recv,
    send,
    recv,
    code_dict_send,
    code_dict_recv,
    code_send,
    code_recv,
    local,
):
    r = lax.axis_index("rows")
    z = lax.axis_index("dict")
    shard = shard_ref.shape[0]
    part = shard // groups
    half = part // 2
    orders = forwarding(groups)
    stages = [arrivals(order) for order in orders]

    def plane(peer):
        return {"rows": peer}

    def column(peer):
        return {"dict": peer}

    barrier = pltpu.get_barrier_semaphore()
    greeted = 0
    for d in range(1, owners):
        pl.semaphore_signal(
            barrier, inc=1, device_id=column(lax.rem(z + d, owners)), device_id_type=pl.DeviceIdType.MESH
        )
        greeted += 1
    for bit in orders[0]:
        pl.semaphore_signal(
            barrier, inc=1, device_id=plane(flipped(r, bit)), device_id_type=pl.DeviceIdType.MESH
        )
        greeted += 1
    pl.semaphore_wait(barrier, greeted)

    def place(owner, group, start, size):
        at = owner * shard + group * part + start
        return pl.ds(pl.multiple_of(at, half), size)

    sent = []

    def to(src, dst, send_sem, recv_sem, peer):
        return pltpu.make_async_remote_copy(
            src_ref=src,
            dst_ref=dst,
            send_sem=send_sem,
            recv_sem=recv_sem,
            device_id=peer,
            device_id_type=pl.DeviceIdType.MESH,
        )

    def relay(src, owner, d, h, upward):
        arrives_as = d + 1 if upward else lax.rem(d + owners - 1, owners)
        lane = arrives_as * 2 + h
        peer = lax.rem(z + (1 if upward else owners - 1), owners)
        return to(
            src,
            out_ref.at[place(owner, r, h * half, half)],
            dict_send.at[lane + (0 if upward else 2 * owners)],
            dict_recv.at[lane],
            column(peer),
        )

    relayed = []

    def relay_if(wanted, *where):
        @pl.when(wanted)
        def _():
            relay(*where).start()

        relayed.append((wanted, where))

    mine = everyone_ref.at[r * owners + z]
    code_first = {}
    code_received = {}

    def forward_codes(src, d, offset, k):
        owner = lax.rem(z + owners - d, owners)
        dst = everyone_ref.at[flipped(r, offset) * owners + owner]
        order = orders[d % 2]
        for later in range(k + 1, len(order)):
            bit = order[later]
            lane = d * groups + (offset ^ bit)
            copy = to(
                dst if src is None else src,
                dst,
                code_send.at[lane],
                code_recv.at[lane],
                plane(flipped(r, bit)),
            )
            copy.start()
            sent.append(copy)
            code_received[d, offset ^ bit] = copy

    def own_half(h):
        return shard_ref.at[pl.ds(pl.multiple_of(r * part + h * half, half), half)]

    for h in range(2):
        relay_if(z + 1 < owners, own_half(h), z, 0, h, True)
        relay_if(z > 0, own_half(h), z, 0, h, False)
    for d in range(1, owners):
        copy = to(
            codes_ref,
            mine,
            code_dict_send.at[d - 1],
            code_dict_recv.at[d - 1],
            column(lax.rem(z + d, owners)),
        )
        copy.start()
        sent.append(copy)
        code_first[d] = copy
    forward_codes(codes_ref, 0, 0, -1)
    own = pltpu.make_async_copy(
        shard_ref, out_ref.at[pl.ds(pl.multiple_of(z * shard, shard), shard)], local.at[0]
    )
    own.start()
    blank = pltpu.make_async_copy(
        zeros_ref, out_ref.at[pl.ds(owners * shard, zeros_ref.shape[0])], local.at[1]
    )
    blank.start()
    own_codes = pltpu.make_async_copy(codes_ref, mine, local.at[2])
    own_codes.start()

    both = jnp.minimum(z, owners - 1 - z)
    longer_below = z > owners - 1 - z

    def arrival(i):
        paired = i < 2 * both
        distance = jnp.where(paired, i // 2 + 1, i - both + 1)
        if i % 2 == 0:
            below = paired | longer_below
        else:
            below = jnp.logical_not(paired) & longer_below
        d = jnp.where(below, distance, owners - distance)
        return d, below

    received = {}

    def forward(i, d, h, index):
        owner = lax.rem(z + owners - d, owners)
        offset, k = stages[h][index]
        where = place(owner, flipped(r, offset), h * half, half)
        for later in range(k + 1, len(orders[h])):
            bit = orders[h][later]
            lane = (i * 2 + h) * groups + (offset ^ bit)
            copy = to(
                out_ref.at[where],
                out_ref.at[where],
                send.at[lane],
                recv.at[lane],
                plane(flipped(r, bit)),
            )
            copy.start()
            sent.append(copy)
            received[i, h, offset ^ bit] = copy

    def plane_step(i, first, last):
        for index in range(first, last):
            for h in range(2):
                received[i, h, stages[h][index][0]].wait_recv()
                forward(i, arrival(i)[0], h, index)

    def code_step(index):
        for d in range(owners):
            offset, k = stages[d % 2][index]
            if index > 0:
                code_received[d, offset].wait_recv()
            elif d > 0:
                code_first[d].wait_recv()
            else:
                continue
            forward_codes(None, d, offset, k)

    for i in range(owners - 1):
        d, below = arrival(i)
        owner = lax.rem(z + owners - d, owners)
        for h in range(2):
            spot = out_ref.at[place(owner, r, h * half, half)]
            to(spot, spot, dict_send.at[0], dict_recv.at[d * 2 + h], column(owner)).wait_recv()
            relay_if(below & (z + 1 < owners), spot, owner, d, h, True)
            relay_if(jnp.logical_not(below) & (z > 0), spot, owner, d, h, False)
            forward(i, d, h, 0)
        if i > 0:
            plane_step(i - 1, 1, groups // 2)
        if i < groups:
            code_step(i)
    plane_step(owners - 2, 1, groups // 2)
    for index in range(owners - 1, groups):
        code_step(index)
    for i in range(owners - 1):
        plane_step(i, groups // 2, groups)
    for copy in sent:
        copy.wait_send()
    for wanted, where in relayed:

        @pl.when(wanted)
        def _():
            relay(*where).wait_send()

    own.wait()
    blank.wait()
    own_codes.wait()


def flipped(r, mask):
    out = r
    bit = 1
    while bit <= mask:
        if mask & bit:
            out = out + bit - 2 * bit * lax.rem(lax.div(r, bit), 2)
        bit *= 2
    return out


def gathered(decoding_table, compacted):
    groups = lax.axis_size("rows")
    owners = lax.axis_size("dict")
    shard, width = decoding_table.shape
    flights = (owners - 1) * 2 * groups
    vmem = pl.BlockSpec(memory_space=pltpu.VMEM)
    anywhere = pl.BlockSpec(memory_space=pl.ANY)
    zeros = jnp.zeros((16, width), decoding_table.dtype)
    return pl.pallas_call(
        functools.partial(table_kernel, groups, owners),
        out_shape=(
            jax.ShapeDtypeStruct((owners * shard + 16, width), decoding_table.dtype),
            jax.ShapeDtypeStruct((owners * groups,) + compacted.shape, compacted.dtype),
        ),
        in_specs=[vmem, vmem, vmem],
        out_specs=(anywhere, anywhere),
        scratch_shapes=[
            pltpu.SemaphoreType.DMA((4 * owners,)),
            pltpu.SemaphoreType.DMA((2 * owners,)),
            pltpu.SemaphoreType.DMA((flights,)),
            pltpu.SemaphoreType.DMA((flights,)),
            pltpu.SemaphoreType.DMA((owners - 1,)),
            pltpu.SemaphoreType.DMA((owners - 1,)),
            pltpu.SemaphoreType.DMA((owners * groups,)),
            pltpu.SemaphoreType.DMA((owners * groups,)),
            pltpu.SemaphoreType.DMA((3,)),
        ],
        compiler_params=pltpu.CompilerParams(
            collective_id=0, has_side_effects=True, vmem_limit_bytes=GRANT
        ),
        cost_estimate=pl.CostEstimate(
            flops=0, bytes_accessed=16 * owners * shard * width, transcendentals=0
        ),
    )(decoding_table, zeros, compacted)


def on_device(lookup_keys_per_record, filter_passed_flags, decoding_table):
    rows_here = lookup_keys_per_record.shape[0]
    shard, width = decoding_table.shape
    rows = rows_here // LANES
    vmem = pl.BlockSpec(memory_space=pltpu.VMEM)
    smem = pl.BlockSpec(memory_space=pltpu.SMEM)

    compacted = pl.pallas_call(
        compact_kernel,
        out_shape=jax.ShapeDtypeStruct((rows + 8, LANES), jnp.int32),
        in_specs=[vmem, vmem],
        out_specs=vmem,
        compiler_params=pltpu.CompilerParams(vmem_limit_bytes=GRANT),
    )(lookup_keys_per_record.reshape(rows, LANES), filter_passed_flags.reshape(rows, LANES))
    table, everyone = gathered(decoding_table, compacted)
    me = lax.axis_index(("rows", "dict")).astype(jnp.int32).reshape(1)
    blank = shard * lax.axis_size("dict")
    blocks = everyone.shape[0]
    return pl.pallas_call(
        functools.partial(decode_kernel, blank),
        out_shape=jax.ShapeDtypeStruct((rows_here, width), decoding_table.dtype),
        in_specs=[smem, vmem, vmem],
        out_specs=vmem,
        scratch_shapes=[
            pltpu.VMEM((rows, LANES), jnp.int32),
            pltpu.VMEM((blocks, LANES), jnp.int32),
            pltpu.VMEM((rows_here, width), jnp.float32),
            pltpu.SMEM((blocks, LANES), jnp.int32),
            pltpu.SMEM((rows, LANES), jnp.int32),
            pltpu.SemaphoreType.DMA((2,)),
        ],
        compiler_params=pltpu.CompilerParams(vmem_limit_bytes=40 * 1024 * 1024),
    )(me, everyone, table.reshape(table.shape[0] // 2, 2, width))


def solution(mesh):
    placed = (P(("rows", "dict")), P(("rows", "dict")), P("dict", None))
    return jax.shard_map(
        on_device, mesh=mesh, in_specs=placed, out_specs=P(("rows", "dict"), None), check_vma=False
    )
```

```python
import functools

import jax
import jax.numpy as jnp
from jax import lax
from jax.experimental import pallas as pl
from jax.experimental.pallas import tpu as pltpu
from jax.sharding import PartitionSpec as P

LANES = 128
GRANT = 12 * 1024 * 1024


def shifted_left(x, step, lane):
    rows = x.shape[0]
    whole, rest = divmod(step, LANES)
    here = pltpu.roll(x, (rows - whole) % rows, 0) if whole % rows else x
    if rest == 0:
        return here
    above = pltpu.roll(here, rows - 1, 0) if rows > 1 else here
    return jnp.where(
        lane < LANES - rest,
        pltpu.roll(here, LANES - rest, 1),
        pltpu.roll(above, LANES - rest, 1),
    )


def running_sum(x, lane, row):
    rows = x.shape[0]
    total = x
    step = 1
    while step < LANES:
        total = total + jnp.where(lane >= step, pltpu.roll(total, step, 1), 0)
        step *= 2
    ends = jnp.broadcast_to(total[:, LANES - 1 :], x.shape)
    before = jnp.where(row >= 1, pltpu.roll(ends, 1, 0), 0)
    step = 1
    while step < rows:
        before = before + jnp.where(row >= step, pltpu.roll(before, step, 0), 0)
        step *= 2
    return total + before


def compact_kernel(codes_ref, flags_ref, out_ref):
    rows = codes_ref.shape[0]
    lane = lax.broadcasted_iota(jnp.int32, (rows, LANES), 1)
    row = lax.broadcasted_iota(jnp.int32, (rows, LANES), 0)
    kept = flags_ref[...] > 0
    sums = running_sum(kept.astype(jnp.int32), lane, row)
    position = row * LANES + lane
    tags = jnp.where(kept, position - sums + 2, 0)
    values = codes_ref[...]
    step = 1
    level = 0
    while step < rows * LANES:
        moving = (tags > 0) & (((tags - 1) >> level) & 1 == 1)
        arrived_tags = shifted_left(jnp.where(moving, tags, 0), step, lane)
        arrived_values = shifted_left(values, step, lane)
        arrives = (arrived_tags > 0) & (position < rows * LANES - step)
        values = jnp.where(arrives, arrived_values, values)
        tags = jnp.where(arrives, arrived_tags, jnp.where(moving, 0, tags))
        step *= 2
        level += 1
    out_ref[:rows, :] = values
    total = jnp.broadcast_to(sums[rows - 1 :, LANES - 1 :], (8, LANES))
    out_ref[rows:, :] = total


def decode_kernel(
    blank, me_ref, codes_ref, table_ref, out_ref, picked, tallies, rows_f32, counts, codes, sem
):
    blocks = codes_ref.shape[0]
    rows = codes_ref.shape[1] - 8
    size = rows * LANES
    lane = lax.broadcasted_iota(jnp.int32, (rows, LANES), 1)
    row = lax.broadcasted_iota(jnp.int32, (rows, LANES), 0)
    position = row * LANES + lane
    tallies[...] = codes_ref[:, rows, :]
    copy = pltpu.make_async_copy(tallies, counts, sem.at[0])
    copy.start()
    picked[...] = jnp.full((rows, LANES), blank, jnp.int32)
    first = me_ref[0] * size
    copy.wait()

    def source(s, start):
        count = counts[s, 0]
        begin = start - first

        @pl.when((begin < size) & (begin + count > 0))
        def _():
            shift = lax.rem(begin + size, size)
            by_row = shift // LANES
            by_lane = lax.rem(shift, LANES)
            moved = pltpu.roll(codes_ref[s, :rows, :], by_row, 0)
            below = pltpu.roll(moved, 1, 0)
            mine = jnp.where(
                lane >= by_lane, pltpu.roll(moved, by_lane, 1), pltpu.roll(below, by_lane, 1)
            )
            inside = (position >= begin) & (position < begin + count)
            picked[...] = jnp.where(inside, mine, picked[...])

        return start + count

    lax.fori_loop(0, blocks, source, jnp.int32(0))
    copy = pltpu.make_async_copy(picked, codes, sem.at[1])
    copy.start()
    copy.wait()

    @pl.loop(0, rows)
    def _(i):
        for j in range(LANES):
            code = codes[i, j]
            pair = table_ref[code >> 1].astype(jnp.float32)
            odd = (code & 1) == 1
            rows_f32[pl.ds(i * LANES + j, 1), :] = jnp.where(odd, pair[1:2], pair[0:1])

    @pl.loop(0, rows)
    def _(i):
        block = pl.ds(pl.multiple_of(i * LANES, LANES), LANES)
        out_ref[block, :] = rows_f32[block, :].astype(out_ref.dtype)


def forwarding(groups):
    bits = [1 << k for k in range(groups.bit_length() - 1)]
    return (bits[1:] + bits[:1], bits[:0:-1] + bits[:1])


def arrivals(order):
    arrived = [(0, -1)]
    for k, bit in enumerate(order):
        arrived += [(e ^ bit, k) for e, _ in arrived]
    return arrived


def table_kernel(
    groups,
    owners,
    shard_ref,
    zeros_ref,
    codes_ref,
    out_ref,
    everyone_ref,
    dict_send,
    dict_recv,
    send,
    recv,
    code_dict_send,
    code_dict_recv,
    code_send,
    code_recv,
    local,
):
    r = lax.axis_index("rows")
    z = lax.axis_index("dict")
    shard = shard_ref.shape[0]
    part = shard // groups
    half = part // 2
    orders = forwarding(groups)
    stages = [arrivals(order) for order in orders]

    def plane(peer):
        return {"rows": peer}

    def column(peer):
        return {"dict": peer}

    barrier = pltpu.get_barrier_semaphore()
    greeted = 0
    for d in range(1, owners):
        pl.semaphore_signal(
            barrier, inc=1, device_id=column(lax.rem(z + d, owners)), device_id_type=pl.DeviceIdType.MESH
        )
        greeted += 1
    for bit in orders[0]:
        pl.semaphore_signal(
            barrier, inc=1, device_id=plane(flipped(r, bit)), device_id_type=pl.DeviceIdType.MESH
        )
        greeted += 1
    pl.semaphore_wait(barrier, greeted)

    def place(owner, group, start, size):
        at = owner * shard + group * part + start
        return pl.ds(pl.multiple_of(at, half), size)

    sent = []

    def to(src, dst, send_sem, recv_sem, peer):
        return pltpu.make_async_remote_copy(
            src_ref=src,
            dst_ref=dst,
            send_sem=send_sem,
            recv_sem=recv_sem,
            device_id=peer,
            device_id_type=pl.DeviceIdType.MESH,
        )

    def relay(src, owner, d, h, upward):
        arrives_as = d + 1 if upward else lax.rem(d + owners - 1, owners)
        lane = arrives_as * 2 + h
        peer = lax.rem(z + (1 if upward else owners - 1), owners)
        return to(
            src,
            out_ref.at[place(owner, r, h * half, half)],
            dict_send.at[lane + (0 if upward else 2 * owners)],
            dict_recv.at[lane],
            column(peer),
        )

    relayed = []

    def relay_if(wanted, *where):
        @pl.when(wanted)
        def _():
            relay(*where).start()

        relayed.append((wanted, where))

    mine = everyone_ref.at[r * owners + z]
    code_first = {}
    code_received = {}

    def forward_codes(src, d, offset, k):
        owner = lax.rem(z + owners - d, owners)
        dst = everyone_ref.at[flipped(r, offset) * owners + owner]
        order = orders[d % 2]
        for later in range(k + 1, len(order)):
            bit = order[later]
            lane = d * groups + (offset ^ bit)
            copy = to(
                dst if src is None else src,
                dst,
                code_send.at[lane],
                code_recv.at[lane],
                plane(flipped(r, bit)),
            )
            copy.start()
            sent.append(copy)
            code_received[d, offset ^ bit] = copy

    def own_half(h):
        return shard_ref.at[pl.ds(pl.multiple_of(r * part + h * half, half), half)]

    for d in range(1, owners):
        copy = to(
            codes_ref,
            mine,
            code_dict_send.at[d - 1],
            code_dict_recv.at[d - 1],
            column(lax.rem(z + d, owners)),
        )
        copy.start()
        sent.append(copy)
        code_first[d] = copy
    forward_codes(codes_ref, 0, 0, -1)
    for h in range(2):
        relay_if(z + 1 < owners, own_half(h), z, 0, h, True)
        relay_if(z > 0, own_half(h), z, 0, h, False)
    own = pltpu.make_async_copy(
        shard_ref, out_ref.at[pl.ds(pl.multiple_of(z * shard, shard), shard)], local.at[0]
    )
    own.start()
    blank = pltpu.make_async_copy(
        zeros_ref, out_ref.at[pl.ds(owners * shard, zeros_ref.shape[0])], local.at[1]
    )
    blank.start()
    own_codes = pltpu.make_async_copy(codes_ref, mine, local.at[2])
    own_codes.start()

    both = jnp.minimum(z, owners - 1 - z)
    longer_below = z > owners - 1 - z

    def arrival(i):
        paired = i < 2 * both
        distance = jnp.where(paired, i // 2 + 1, i - both + 1)
        if i % 2 == 0:
            below = paired | longer_below
        else:
            below = jnp.logical_not(paired) & longer_below
        d = jnp.where(below, distance, owners - distance)
        return d, below

    received = {}

    def forward(i, d, h, index):
        owner = lax.rem(z + owners - d, owners)
        offset, k = stages[h][index]
        where = place(owner, flipped(r, offset), h * half, half)
        for later in range(k + 1, len(orders[h])):
            bit = orders[h][later]
            lane = (i * 2 + h) * groups + (offset ^ bit)
            copy = to(
                out_ref.at[where],
                out_ref.at[where],
                send.at[lane],
                recv.at[lane],
                plane(flipped(r, bit)),
            )
            copy.start()
            sent.append(copy)
            received[i, h, offset ^ bit] = copy

    def plane_step(i, first, last):
        for index in range(first, last):
            for h in range(2):
                received[i, h, stages[h][index][0]].wait_recv()
                forward(i, arrival(i)[0], h, index)

    def code_step(index):
        for d in range(owners):
            offset, k = stages[d % 2][index]
            if index > 0:
                code_received[d, offset].wait_recv()
            elif d > 0:
                code_first[d].wait_recv()
            else:
                continue
            forward_codes(None, d, offset, k)

    code_step(0)
    for i in range(owners - 1):
        d, below = arrival(i)
        owner = lax.rem(z + owners - d, owners)
        for h in range(2):
            spot = out_ref.at[place(owner, r, h * half, half)]
            to(spot, spot, dict_send.at[0], dict_recv.at[d * 2 + h], column(owner)).wait_recv()
            relay_if(below & (z + 1 < owners), spot, owner, d, h, True)
            relay_if(jnp.logical_not(below) & (z > 0), spot, owner, d, h, False)
            forward(i, d, h, 0)
        if i > 0:
            plane_step(i - 1, 1, groups // 2)
        if i == 0:
            code_step(1)
        if i == 1:
            for index in range(2, groups // 2):
                code_step(index)
    plane_step(owners - 2, 1, groups // 2)
    for index in range(groups // 2, groups):
        code_step(index)
    for i in range(owners - 1):
        plane_step(i, groups // 2, groups)
    for copy in sent:
        copy.wait_send()
    for wanted, where in relayed:

        @pl.when(wanted)
        def _():
            relay(*where).wait_send()

    own.wait()
    blank.wait()
    own_codes.wait()


def flipped(r, mask):
    out = r
    bit = 1
    while bit <= mask:
        if mask & bit:
            out = out + bit - 2 * bit * lax.rem(lax.div(r, bit), 2)
        bit *= 2
    return out


def gathered(decoding_table, compacted):
    groups = lax.axis_size("rows")
    owners = lax.axis_size("dict")
    shard, width = decoding_table.shape
    flights = (owners - 1) * 2 * groups
    vmem = pl.BlockSpec(memory_space=pltpu.VMEM)
    anywhere = pl.BlockSpec(memory_space=pl.ANY)
    zeros = jnp.zeros((16, width), decoding_table.dtype)
    return pl.pallas_call(
        functools.partial(table_kernel, groups, owners),
        out_shape=(
            jax.ShapeDtypeStruct((owners * shard + 16, width), decoding_table.dtype),
            jax.ShapeDtypeStruct((owners * groups,) + compacted.shape, compacted.dtype),
        ),
        in_specs=[vmem, vmem, vmem],
        out_specs=(anywhere, anywhere),
        scratch_shapes=[
            pltpu.SemaphoreType.DMA((4 * owners,)),
            pltpu.SemaphoreType.DMA((2 * owners,)),
            pltpu.SemaphoreType.DMA((flights,)),
            pltpu.SemaphoreType.DMA((flights,)),
            pltpu.SemaphoreType.DMA((owners - 1,)),
            pltpu.SemaphoreType.DMA((owners - 1,)),
            pltpu.SemaphoreType.DMA((owners * groups,)),
            pltpu.SemaphoreType.DMA((owners * groups,)),
            pltpu.SemaphoreType.DMA((3,)),
        ],
        compiler_params=pltpu.CompilerParams(
            collective_id=0, has_side_effects=True, vmem_limit_bytes=GRANT
        ),
        cost_estimate=pl.CostEstimate(
            flops=0, bytes_accessed=16 * owners * shard * width, transcendentals=0
        ),
    )(decoding_table, zeros, compacted)


def on_device(lookup_keys_per_record, filter_passed_flags, decoding_table):
    rows_here = lookup_keys_per_record.shape[0]
    shard, width = decoding_table.shape
    rows = rows_here // LANES
    vmem = pl.BlockSpec(memory_space=pltpu.VMEM)
    smem = pl.BlockSpec(memory_space=pltpu.SMEM)

    compacted = pl.pallas_call(
        compact_kernel,
        out_shape=jax.ShapeDtypeStruct((rows + 8, LANES), jnp.int32),
        in_specs=[vmem, vmem],
        out_specs=vmem,
        compiler_params=pltpu.CompilerParams(vmem_limit_bytes=GRANT),
    )(lookup_keys_per_record.reshape(rows, LANES), filter_passed_flags.reshape(rows, LANES))
    table, everyone = gathered(decoding_table, compacted)
    me = lax.axis_index(("rows", "dict")).astype(jnp.int32).reshape(1)
    blank = shard * lax.axis_size("dict")
    blocks = everyone.shape[0]
    return pl.pallas_call(
        functools.partial(decode_kernel, blank),
        out_shape=jax.ShapeDtypeStruct((rows_here, width), decoding_table.dtype),
        in_specs=[smem, vmem, vmem],
        out_specs=vmem,
        scratch_shapes=[
            pltpu.VMEM((rows, LANES), jnp.int32),
            pltpu.VMEM((blocks, LANES), jnp.int32),
            pltpu.VMEM((rows_here, width), jnp.float32),
            pltpu.SMEM((blocks, LANES), jnp.int32),
            pltpu.SMEM((rows, LANES), jnp.int32),
            pltpu.SemaphoreType.DMA((2,)),
        ],
        compiler_params=pltpu.CompilerParams(vmem_limit_bytes=40 * 1024 * 1024),
    )(me, everyone, table.reshape(table.shape[0] // 2, 2, width))


def solution(mesh):
    placed = (P(("rows", "dict")), P(("rows", "dict")), P("dict", None))
    return jax.shard_map(
        on_device, mesh=mesh, in_specs=placed, out_specs=P(("rows", "dict"), None), check_vma=False
    )
```

```python
import functools

import jax
import jax.numpy as jnp
from jax import lax
from jax.experimental import pallas as pl
from jax.experimental.pallas import tpu as pltpu
from jax.sharding import PartitionSpec as P

LANES = 128
GRANT = 12 * 1024 * 1024


def shifted_left(x, step, lane):
    rows = x.shape[0]
    whole, rest = divmod(step, LANES)
    here = pltpu.roll(x, (rows - whole) % rows, 0) if whole % rows else x
    if rest == 0:
        return here
    above = pltpu.roll(here, rows - 1, 0) if rows > 1 else here
    return jnp.where(
        lane < LANES - rest,
        pltpu.roll(here, LANES - rest, 1),
        pltpu.roll(above, LANES - rest, 1),
    )


def running_sum(x, lane, row):
    rows = x.shape[0]
    total = x
    step = 1
    while step < LANES:
        total = total + jnp.where(lane >= step, pltpu.roll(total, step, 1), 0)
        step *= 2
    ends = jnp.broadcast_to(total[:, LANES - 1 :], x.shape)
    before = jnp.where(row >= 1, pltpu.roll(ends, 1, 0), 0)
    step = 1
    while step < rows:
        before = before + jnp.where(row >= step, pltpu.roll(before, step, 0), 0)
        step *= 2
    return total + before


def compact_kernel(codes_ref, flags_ref, out_ref):
    rows = codes_ref.shape[0]
    lane = lax.broadcasted_iota(jnp.int32, (rows, LANES), 1)
    row = lax.broadcasted_iota(jnp.int32, (rows, LANES), 0)
    kept = flags_ref[...] > 0
    sums = running_sum(kept.astype(jnp.int32), lane, row)
    position = row * LANES + lane
    tags = jnp.where(kept, position - sums + 2, 0)
    values = codes_ref[...]
    step = 1
    level = 0
    while step < rows * LANES:
        moving = (tags > 0) & (((tags - 1) >> level) & 1 == 1)
        arrived_tags = shifted_left(jnp.where(moving, tags, 0), step, lane)
        arrived_values = shifted_left(values, step, lane)
        arrives = (arrived_tags > 0) & (position < rows * LANES - step)
        values = jnp.where(arrives, arrived_values, values)
        tags = jnp.where(arrives, arrived_tags, jnp.where(moving, 0, tags))
        step *= 2
        level += 1
    out_ref[:rows, :] = values
    total = jnp.broadcast_to(sums[rows - 1 :, LANES - 1 :], (8, LANES))
    out_ref[rows:, :] = total


def decode_kernel(
    blank, me_ref, codes_ref, table_ref, out_ref, picked, tallies, rows_f32, counts, codes, sem
):
    blocks = codes_ref.shape[0]
    rows = codes_ref.shape[1] - 8
    size = rows * LANES
    lane = lax.broadcasted_iota(jnp.int32, (rows, LANES), 1)
    row = lax.broadcasted_iota(jnp.int32, (rows, LANES), 0)
    position = row * LANES + lane
    tallies[...] = codes_ref[:, rows, :]
    copy = pltpu.make_async_copy(tallies, counts, sem.at[0])
    copy.start()
    picked[...] = jnp.full((rows, LANES), blank, jnp.int32)
    first = me_ref[0] * size
    copy.wait()

    def source(s, start):
        count = counts[s, 0]
        begin = start - first

        @pl.when((begin < size) & (begin + count > 0))
        def _():
            shift = lax.rem(begin + size, size)
            by_row = shift // LANES
            by_lane = lax.rem(shift, LANES)
            moved = pltpu.roll(codes_ref[s, :rows, :], by_row, 0)
            below = pltpu.roll(moved, 1, 0)
            mine = jnp.where(
                lane >= by_lane, pltpu.roll(moved, by_lane, 1), pltpu.roll(below, by_lane, 1)
            )
            inside = (position >= begin) & (position < begin + count)
            picked[...] = jnp.where(inside, mine, picked[...])

        return start + count

    lax.fori_loop(0, blocks, source, jnp.int32(0))
    copy = pltpu.make_async_copy(picked, codes, sem.at[1])
    copy.start()
    copy.wait()

    @pl.loop(0, rows)
    def _(i):
        for j in range(LANES):
            code = codes[i, j]
            pair = table_ref[code >> 1].astype(jnp.float32)
            odd = (code & 1) == 1
            rows_f32[pl.ds(i * LANES + j, 1), :] = jnp.where(odd, pair[1:2], pair[0:1])

    @pl.loop(0, rows)
    def _(i):
        block = pl.ds(pl.multiple_of(i * LANES, LANES), LANES)
        out_ref[block, :] = rows_f32[block, :].astype(out_ref.dtype)


def forwarding(groups):
    bits = [1 << k for k in range(groups.bit_length() - 1)]
    return (bits[1:] + bits[:1], bits[:0:-1] + bits[:1])


def arrivals(order):
    arrived = [(0, -1)]
    for k, bit in enumerate(order):
        arrived += [(e ^ bit, k) for e, _ in arrived]
    return arrived


def table_kernel(
    groups,
    owners,
    shard_ref,
    zeros_ref,
    codes_ref,
    out_ref,
    everyone_ref,
    dict_send,
    dict_recv,
    send,
    recv,
    code_dict_send,
    code_dict_recv,
    code_send,
    code_recv,
    local,
):
    r = lax.axis_index("rows")
    z = lax.axis_index("dict")
    shard = shard_ref.shape[0]
    part = shard // groups
    half = part // 2
    orders = forwarding(groups)
    stages = [arrivals(order) for order in orders]

    def plane(peer):
        return {"rows": peer}

    def column(peer):
        return {"dict": peer}

    barrier = pltpu.get_barrier_semaphore()
    greeted = 0
    for d in range(1, owners):
        pl.semaphore_signal(
            barrier, inc=1, device_id=column(lax.rem(z + d, owners)), device_id_type=pl.DeviceIdType.MESH
        )
        greeted += 1
    for bit in orders[0]:
        pl.semaphore_signal(
            barrier, inc=1, device_id=plane(flipped(r, bit)), device_id_type=pl.DeviceIdType.MESH
        )
        greeted += 1
    pl.semaphore_wait(barrier, greeted)

    def place(owner, group, start, size):
        at = owner * shard + group * part + start
        return pl.ds(pl.multiple_of(at, half), size)

    sent = []

    def to(src, dst, send_sem, recv_sem, peer):
        return pltpu.make_async_remote_copy(
            src_ref=src,
            dst_ref=dst,
            send_sem=send_sem,
            recv_sem=recv_sem,
            device_id=peer,
            device_id_type=pl.DeviceIdType.MESH,
        )

    def relay(src, owner, d, h, upward):
        arrives_as = d + 1 if upward else lax.rem(d + owners - 1, owners)
        lane = arrives_as * 2 + h
        peer = lax.rem(z + (1 if upward else owners - 1), owners)
        return to(
            src,
            out_ref.at[place(owner, r, h * half, half)],
            dict_send.at[lane + (0 if upward else 2 * owners)],
            dict_recv.at[lane],
            column(peer),
        )

    relayed = []

    def relay_if(wanted, *where):
        @pl.when(wanted)
        def _():
            relay(*where).start()

        relayed.append((wanted, where))

    mine = everyone_ref.at[r * owners + z]
    code_first = {}
    code_received = {}

    def forward_codes(src, d, offset, k):
        owner = lax.rem(z + owners - d, owners)
        dst = everyone_ref.at[flipped(r, offset) * owners + owner]
        order = orders[d % 2]
        for later in range(k + 1, len(order)):
            bit = order[later]
            lane = d * groups + (offset ^ bit)
            copy = to(
                dst if src is None else src,
                dst,
                code_send.at[lane],
                code_recv.at[lane],
                plane(flipped(r, bit)),
            )
            copy.start()
            sent.append(copy)
            code_received[d, offset ^ bit] = copy

    def own_half(h):
        return shard_ref.at[pl.ds(pl.multiple_of(r * part + h * half, half), half)]

    for h in range(2):
        relay_if(z + 1 < owners, own_half(h), z, 0, h, True)
        relay_if(z > 0, own_half(h), z, 0, h, False)
    for d in range(1, owners):
        copy = to(
            codes_ref,
            mine,
            code_dict_send.at[d - 1],
            code_dict_recv.at[d - 1],
            column(lax.rem(z + d, owners)),
        )
        copy.start()
        sent.append(copy)
        code_first[d] = copy
    forward_codes(codes_ref, 0, 0, -1)
    own = pltpu.make_async_copy(
        shard_ref, out_ref.at[pl.ds(pl.multiple_of(z * shard, shard), shard)], local.at[0]
    )
    blank = pltpu.make_async_copy(
        zeros_ref, out_ref.at[pl.ds(owners * shard, zeros_ref.shape[0])], local.at[1]
    )
    blank.start()
    own_codes = pltpu.make_async_copy(codes_ref, mine, local.at[2])
    own_codes.start()

    both = jnp.minimum(z, owners - 1 - z)
    longer_below = z > owners - 1 - z

    def arrival(i):
        paired = i < 2 * both
        distance = jnp.where(paired, i // 2 + 1, i - both + 1)
        if i % 2 == 0:
            below = paired | longer_below
        else:
            below = jnp.logical_not(paired) & longer_below
        d = jnp.where(below, distance, owners - distance)
        return d, below

    received = {}

    def forward(i, d, h, index):
        owner = lax.rem(z + owners - d, owners)
        offset, k = stages[h][index]
        where = place(owner, flipped(r, offset), h * half, half)
        for later in range(k + 1, len(orders[h])):
            bit = orders[h][later]
            lane = (i * 2 + h) * groups + (offset ^ bit)
            copy = to(
                out_ref.at[where],
                out_ref.at[where],
                send.at[lane],
                recv.at[lane],
                plane(flipped(r, bit)),
            )
            copy.start()
            sent.append(copy)
            received[i, h, offset ^ bit] = copy

    def plane_step(i, first, last):
        for index in range(first, last):
            for h in range(2):
                received[i, h, stages[h][index][0]].wait_recv()
                forward(i, arrival(i)[0], h, index)

    def code_step(index):
        for d in range(owners):
            offset, k = stages[d % 2][index]
            if index > 0:
                code_received[d, offset].wait_recv()
            elif d > 0:
                code_first[d].wait_recv()
            else:
                continue
            forward_codes(None, d, offset, k)

    for i in range(owners - 1):
        d, below = arrival(i)
        owner = lax.rem(z + owners - d, owners)
        for h in range(2):
            spot = out_ref.at[place(owner, r, h * half, half)]
            to(spot, spot, dict_send.at[0], dict_recv.at[d * 2 + h], column(owner)).wait_recv()
            relay_if(below & (z + 1 < owners), spot, owner, d, h, True)
            relay_if(jnp.logical_not(below) & (z > 0), spot, owner, d, h, False)
            forward(i, d, h, 0)
        if i == 0:
            own.start()
        if i > 0:
            plane_step(i - 1, 1, groups // 2)
        if i < groups:
            code_step(i)
    plane_step(owners - 2, 1, groups // 2)
    for index in range(owners - 1, groups):
        code_step(index)
    for i in range(owners - 1):
        plane_step(i, groups // 2, groups)
    for copy in sent:
        copy.wait_send()
    for wanted, where in relayed:

        @pl.when(wanted)
        def _():
            relay(*where).wait_send()

    own.wait()
    blank.wait()
    own_codes.wait()


def flipped(r, mask):
    out = r
    bit = 1
    while bit <= mask:
        if mask & bit:
            out = out + bit - 2 * bit * lax.rem(lax.div(r, bit), 2)
        bit *= 2
    return out


def gathered(decoding_table, compacted):
    groups = lax.axis_size("rows")
    owners = lax.axis_size("dict")
    shard, width = decoding_table.shape
    flights = (owners - 1) * 2 * groups
    vmem = pl.BlockSpec(memory_space=pltpu.VMEM)
    anywhere = pl.BlockSpec(memory_space=pl.ANY)
    zeros = jnp.zeros((16, width), decoding_table.dtype)
    return pl.pallas_call(
        functools.partial(table_kernel, groups, owners),
        out_shape=(
            jax.ShapeDtypeStruct((owners * shard + 16, width), decoding_table.dtype),
            jax.ShapeDtypeStruct((owners * groups,) + compacted.shape, compacted.dtype),
        ),
        in_specs=[pl.BlockSpec(memory_space=pltpu.HBM), vmem, vmem],
        out_specs=(anywhere, anywhere),
        scratch_shapes=[
            pltpu.SemaphoreType.DMA((4 * owners,)),
            pltpu.SemaphoreType.DMA((2 * owners,)),
            pltpu.SemaphoreType.DMA((flights,)),
            pltpu.SemaphoreType.DMA((flights,)),
            pltpu.SemaphoreType.DMA((owners - 1,)),
            pltpu.SemaphoreType.DMA((owners - 1,)),
            pltpu.SemaphoreType.DMA((owners * groups,)),
            pltpu.SemaphoreType.DMA((owners * groups,)),
            pltpu.SemaphoreType.DMA((3,)),
        ],
        compiler_params=pltpu.CompilerParams(
            collective_id=0, has_side_effects=True, vmem_limit_bytes=GRANT
        ),
        cost_estimate=pl.CostEstimate(
            flops=0, bytes_accessed=16 * owners * shard * width, transcendentals=0
        ),
    )(decoding_table, zeros, compacted)


def on_device(lookup_keys_per_record, filter_passed_flags, decoding_table):
    rows_here = lookup_keys_per_record.shape[0]
    shard, width = decoding_table.shape
    rows = rows_here // LANES
    vmem = pl.BlockSpec(memory_space=pltpu.VMEM)
    smem = pl.BlockSpec(memory_space=pltpu.SMEM)

    compacted = pl.pallas_call(
        compact_kernel,
        out_shape=jax.ShapeDtypeStruct((rows + 8, LANES), jnp.int32),
        in_specs=[vmem, vmem],
        out_specs=vmem,
        compiler_params=pltpu.CompilerParams(vmem_limit_bytes=GRANT),
    )(lookup_keys_per_record.reshape(rows, LANES), filter_passed_flags.reshape(rows, LANES))
    table, everyone = gathered(decoding_table, compacted)
    me = lax.axis_index(("rows", "dict")).astype(jnp.int32).reshape(1)
    blank = shard * lax.axis_size("dict")
    blocks = everyone.shape[0]
    return pl.pallas_call(
        functools.partial(decode_kernel, blank),
        out_shape=jax.ShapeDtypeStruct((rows_here, width), decoding_table.dtype),
        in_specs=[smem, vmem, vmem],
        out_specs=vmem,
        scratch_shapes=[
            pltpu.VMEM((rows, LANES), jnp.int32),
            pltpu.VMEM((blocks, LANES), jnp.int32),
            pltpu.VMEM((rows_here, width), jnp.float32),
            pltpu.SMEM((blocks, LANES), jnp.int32),
            pltpu.SMEM((rows, LANES), jnp.int32),
            pltpu.SemaphoreType.DMA((2,)),
        ],
        compiler_params=pltpu.CompilerParams(vmem_limit_bytes=40 * 1024 * 1024),
    )(me, everyone, table.reshape(table.shape[0] // 2, 2, width))


def solution(mesh):
    placed = (P(("rows", "dict")), P(("rows", "dict")), P("dict", None))
    return jax.shard_map(
        on_device, mesh=mesh, in_specs=placed, out_specs=P(("rows", "dict"), None), check_vma=False
    )
```
